512 devices in a mesh: expert: 128 (over z, y, core), help: 4 (over x).
Axes of the slice: x: 4, y: 4, z: 16, core: 2. Of those that a mesh axis runs over, the one named last changes fastest.
Arguments:
- act_rows: bfloat16 [65536, 1536], P(('expert', 'help')), may hold values from -1.1953125 to 1.1953125
- grad_rows: bfloat16 [65536, 4096], P(('expert', 'help')), may hold values from -1.1953125 to 1.1953125
- routing: int32 [65536], P(('expert', 'help')), may hold values from 0 to 127, as said below
- input_panel: bfloat16 [128, 1536, 512], P('expert', None, 'help'), may hold values from -0.15625 to 0.15625
- output_panel: bfloat16 [128, 4096, 1024], P('expert', None, 'help'), may hold values from -0.09375 to 0.09375
Outputs:
- scaling: float32 [128, 512, 1024], P('expert', None, 'help')
The draws below stay inside these ranges and needn't reach their ends.
Inputs may be any that keep to these rules, and one draw needn't show every extreme that they name: `routing`: among the rows of one device (aligned blocks of 128 rows), no expert is named more than 2 times, and one expert, the same on every device, is named exactly 2 times on every device.
All inputs are finite; a program needn't handle non-finite values.
Results may differ from the reference program's by a relative error of at most 0.00083.
Values may be sent and summed in bfloat16 or wider, within the bound.
No kernel may reach another device: no remote copies, remote signals or barrier semaphores. Data moves between devices by JAX's collectives and lax.ppermute only.
A program may use at most 64 MiB of HBM per device.

```python
import jax
import jax.numpy as jnp
from jax import lax

D = 4096
FF = 1536
A_PAN = 512
G_PAN = 1024
ROWS_DEV = 128
EXPERTS = 128
CAP = 2
ROWS = 65536
N_EXPERT = 128
N_HELP = 4


def draw_routing(key, part):
    blocks = ROWS // ROWS_DEV
    slot_total = EXPERTS * CAP
    key_hot, key_weight, key_noise, key_order = jax.random.split(jax.random.fold_in(key, 17), 4)
    hot_expert = jax.random.randint(key_hot, (), 0, EXPERTS)
    expert_weight = jax.random.randint(key_weight, (EXPERTS,), 0, 4096)
    noise = jax.random.randint(key_noise, (blocks, slot_total), 0, 4096)
    slot_index = jnp.arange(slot_total, dtype=jnp.int32)
    slot_expert = slot_index // CAP
    score = (noise + expert_weight[slot_expert][None, :]) * slot_total + slot_index[None, :]
    score = jnp.where((slot_expert == hot_expert)[None, :], -1 - slot_index[None, :], score)
    unused, picked = lax.top_k(score, ROWS_DEV - CAP)
    chosen = jnp.concatenate([jnp.full((blocks, CAP), hot_expert, jnp.int32), slot_expert[picked].astype(jnp.int32)], axis=1)
    shuffles = jax.vmap(lambda k: jax.random.permutation(k, ROWS_DEV))(jax.random.split(key_order, blocks))
    chosen = jnp.take_along_axis(chosen, shuffles, axis=1)
    return chosen.reshape(ROWS).astype(jnp.int32)


def steps_of(own_key, shape, cuts, low, largest):
    factor_of = 1.0
    for position, parts in cuts:
        draws = jax.random.uniform(jax.random.fold_in(jax.random.fold_in(own_key, 6), position), (parts,), jnp.float32, low / len(cuts), largest / len(cuts))
        factor_of = factor_of * jnp.repeat(jnp.exp(draws), shape[position] // parts).reshape((-1,) + (1,) * (len(shape) - 1 - position))
    return factor_of


def bell_draw(stream_key, shape, width, most, pieces=(), held_as=jnp.bfloat16):
    gain = steps_of(stream_key, shape, pieces, -0.22, 0.18) if pieces else 1.0
    values = jax.random.normal(stream_key, shape, jnp.float32) * width * gain
    return jnp.minimum(jnp.maximum(values, -most), most).astype(held_as)


def setup_inputs(seed: int = 0) -> dict:
    splits = jax.random.split(jax.random.key(seed), 6)
    return {
        "act_rows": bell_draw(splits[0], (ROWS, FF), 0.2, 1.1953125, ((0, 512),)),
        "grad_rows": bell_draw(splits[1], (ROWS, D), 0.2, 1.1953125, ((0, 512),)),
        "routing": draw_routing(jax.random.fold_in(splits[5], 71), 0),
        "input_panel": bell_draw(splits[3], (EXPERTS, FF, A_PAN), FF ** -0.5, 0.15625, ((0, 128), (2, 4))),
        "output_panel": bell_draw(splits[4], (EXPERTS, D, G_PAN), D ** -0.5, 0.09375, ((0, 128), (2, 4))),
    }


def reference(act_rows, grad_rows, routing, input_panel, output_panel):
    most_rows = CAP * N_EXPERT * N_HELP
    ordering = jnp.argsort(routing, stable=True).astype(jnp.int32)
    expert_ids = jnp.arange(EXPERTS, dtype=jnp.int32)
    expert_load = jnp.sum((routing[None, :] == expert_ids[:, None]).astype(jnp.int32), axis=1).astype(jnp.int32)
    expert_start = (jnp.cumsum(expert_load) - expert_load).astype(jnp.int32)
    sorted_input = jnp.concatenate([act_rows[ordering], jnp.zeros((most_rows, FF), act_rows.dtype)], axis=0)
    sorted_grad = jnp.concatenate([grad_rows[ordering], jnp.zeros((most_rows, D), grad_rows.dtype)], axis=0)

    def refit_expert(expert):
        start = expert_start[expert]
        input_block = lax.dynamic_slice_in_dim(sorted_input, start, most_rows, 0).astype(jnp.float32)
        grad_block = lax.dynamic_slice_in_dim(sorted_grad, start, most_rows, 0).astype(jnp.float32)
        live = jnp.arange(most_rows, dtype=jnp.int32) < expert_load[expert]
        input_rot = jnp.dot(input_block, input_panel[expert].astype(jnp.float32), precision=lax.Precision.HIGHEST)
        grad_rot = jnp.dot(grad_block, output_panel[expert].astype(jnp.float32), precision=lax.Precision.HIGHEST)
        input_squares = jnp.where(live[:, None], jnp.square(input_rot), 0.0).astype(jnp.bfloat16)
        grad_squares = jnp.where(live[:, None], jnp.square(grad_rot), 0.0).astype(jnp.bfloat16)
        return jnp.dot(input_squares.astype(jnp.float32).T, grad_squares.astype(jnp.float32), precision=lax.Precision.HIGHEST)

    return lax.map(refit_expert, expert_ids)
```

```python
import jax
import jax.numpy as jnp
from jax import lax
from jax.experimental import pallas as pl
from jax.experimental.pallas import tpu as pltpu
from jax.sharding import PartitionSpec as P


def shifted(values, steps):
    helpers = lax.axis_size("help")
    return lax.ppermute(values, "help", [(i, (i + steps) % helpers) for i in range(helpers)])


def tile_kernel(helpers, me_ref, *refs):
    in_refs, out_refs, tile_ref = refs[:helpers], refs[helpers:-1], refs[-1]
    width = in_refs[0].shape[1] // helpers
    me = me_ref[0]
    for j in range(helpers):
        total = None
        for k in range(helpers):
            block = (j + k) % helpers
            term = lax.dot_general(
                in_refs[k][:, block * width : (block + 1) * width],
                out_refs[k][...],
                (((0,), (0,)), ((), ())),
                preferred_element_type=jnp.float32,
            )
            total = term if total is None else total + term
        start = pl.multiple_of(lax.rem(me + helpers - j, helpers) * width, width)
        tile_ref[0, pl.ds(start, width), :] = total


def on_device(act_rows, grad_rows, routing, input_panel, output_panel):
    row_count = routing.shape[0]
    experts = lax.axis_size("expert")
    helpers = lax.axis_size("help")
    width_in, width_out = act_rows.shape[1], grad_rows.shape[1]

    row_index = jnp.arange(row_count, dtype=jnp.int32)
    earlier = (routing[:, None] == routing[None, :]) & (row_index[:, None] < row_index[None, :])
    rank = jnp.sum(earlier.astype(jnp.int32), axis=0)
    target = routing * 2 + rank
    pick = (jnp.arange(experts * 2, dtype=jnp.int32)[:, None] == target[None, :]).astype(jnp.bfloat16)
    rows = jnp.concatenate([grad_rows, act_rows], axis=1)
    send = jnp.dot(pick, rows, preferred_element_type=jnp.float32).astype(jnp.bfloat16)
    send = send.reshape(experts, 2, width_in + width_out)
    arrived = lax.all_to_all(send, "expert", split_axis=0, concat_axis=0, tiled=True)
    arrived = arrived.reshape(experts * 2, width_in + width_out)

    in_parts = [input_panel[0]] + [shifted(input_panel[0], k) for k in range(1, helpers)]
    out_parts = [output_panel[0]] + [shifted(output_panel[0], k) for k in range(1, helpers)]

    def squares(values, panel):
        return jnp.square(jnp.dot(values, panel, preferred_element_type=jnp.float32)).astype(jnp.bfloat16)

    own_in = jnp.concatenate([squares(arrived[:, width_out:], part) for part in in_parts], axis=1)
    own_out = [squares(arrived[:, :width_out], part) for part in out_parts]
    all_in = [own_in] + [shifted(own_in, helpers - k) for k in range(1, helpers)]
    all_out = [own_out[0]] + [shifted(own_out[k], helpers - k) for k in range(1, helpers)]

    panel_in, panel_out = own_in.shape[1], own_out[0].shape[1]
    me = lax.axis_index("help").astype(jnp.int32)[None]
    return pl.pallas_call(
        lambda *refs: tile_kernel(helpers, *refs),
        out_shape=jax.ShapeDtypeStruct((1, panel_in, panel_out), jnp.float32),
        in_specs=[pl.BlockSpec(memory_space=pltpu.SMEM)] + [pl.BlockSpec(memory_space=pltpu.VMEM)] * (2 * helpers),
        out_specs=pl.BlockSpec(memory_space=pltpu.VMEM),
        name="tile",
    )(me, *all_in, *all_out)


def solution(mesh):
    placed = (
        P(("expert", "help"), None),
        P(("expert", "help"), None),
        P(("expert", "help")),
        P("expert", None, "help"),
        P("expert", None, "help"),
    )
    return jax.shard_map(
        on_device, mesh=mesh, in_specs=placed, out_specs=P("expert", None, "help"), check_vma=False
    )
```

```python
import jax
import jax.numpy as jnp
from jax import lax
from jax.experimental import pallas as pl
from jax.experimental.pallas import tpu as pltpu
from jax.sharding import PartitionSpec as P


def shifted(values, steps):
    helpers = lax.axis_size("help")
    return lax.ppermute(values, "help", [(i, (i + steps) % helpers) for i in range(helpers)])


def tile_kernel(helpers, me_ref, *refs):
    in_refs, out_refs, tile_ref = refs[:helpers], refs[helpers:-1], refs[-1]
    width = in_refs[0].shape[1] // helpers
    me = me_ref[0]
    for j in range(helpers):
        total = None
        for k in range(helpers):
            block = (j + k) % helpers
            term = lax.dot_general(
                in_refs[k][:, block * width : (block + 1) * width],
                out_refs[k][...],
                (((0,), (0,)), ((), ())),
                preferred_element_type=jnp.float32,
            )
            total = term if total is None else total + term
        start = pl.multiple_of(lax.rem(me + helpers - j, helpers) * width, width)
        tile_ref[0, pl.ds(start, width), :] = total


def on_device(act_rows, grad_rows, routing, input_panel, output_panel):
    row_count = routing.shape[0]
    experts = lax.axis_size("expert")
    helpers = lax.axis_size("help")
    width_in, width_out = act_rows.shape[1], grad_rows.shape[1]

    row_index = jnp.arange(row_count, dtype=jnp.int32)
    earlier = (routing[:, None] == routing[None, :]) & (row_index[:, None] < row_index[None, :])
    rank = jnp.sum(earlier.astype(jnp.int32), axis=0)
    target = routing * 2 + rank
    pick = (jnp.arange(experts * 2, dtype=jnp.int32)[:, None] == target[None, :]).astype(jnp.bfloat16)
    rows = jnp.concatenate([grad_rows, act_rows], axis=1)
    send = jnp.dot(pick, rows, preferred_element_type=jnp.float32).astype(jnp.bfloat16)
    send = send.reshape(experts, 2, width_in + width_out)
    arrived = lax.all_to_all(send, "expert", split_axis=0, concat_axis=0, tiled=True)
    arrived = arrived.reshape(experts * 2, width_in + width_out)

    in_parts = [input_panel[0]] + [shifted(input_panel[0], k) for k in range(1, helpers)]
    out_parts = [output_panel[0]] + [shifted(output_panel[0], k) for k in range(1, helpers)]

    def squares(values, panel):
        return jnp.square(jnp.dot(values, panel, preferred_element_type=jnp.float32)).astype(jnp.bfloat16)

    joined_in, joined_out = jnp.concatenate(in_parts, axis=1), jnp.concatenate(out_parts, axis=1)
    joined_in, joined_out, arrived = lax.optimization_barrier((joined_in, joined_out, arrived))
    own_in = squares(arrived[:, width_out:], joined_in)
    all_out = squares(arrived[:, :width_out], joined_out)
    part_out = output_panel.shape[2]
    own_out = [all_out[:, k * part_out : (k + 1) * part_out] for k in range(helpers)]
    all_in = [own_in] + [shifted(own_in, helpers - k) for k in range(1, helpers)]
    all_out = [own_out[0]] + [shifted(own_out[k], helpers - k) for k in range(1, helpers)]

    panel_in, panel_out = own_in.shape[1], own_out[0].shape[1]
    me = lax.axis_index("help").astype(jnp.int32)[None]
    return pl.pallas_call(
        lambda *refs: tile_kernel(helpers, *refs),
        out_shape=jax.ShapeDtypeStruct((1, panel_in, panel_out), jnp.float32),
        in_specs=[pl.BlockSpec(memory_space=pltpu.SMEM)] + [pl.BlockSpec(memory_space=pltpu.VMEM)] * (2 * helpers),
        out_specs=pl.BlockSpec(memory_space=pltpu.VMEM),
        compiler_params=pltpu.CompilerParams(vmem_limit_bytes=16 * 1024 * 1024),
        name="tile",
    )(me, *all_in, *all_out)


def solution(mesh):
    placed = (
        P(("expert", "help"), None),
        P(("expert", "help"), None),
        P(("expert", "help")),
        P("expert", None, "help"),
        P("expert", None, "help"),
    )
    return jax.shard_map(
        on_device, mesh=mesh, in_specs=placed, out_specs=P("expert", None, "help"), check_vma=False
    )
```

```python
import functools

import jax
import jax.numpy as jnp
from jax import lax
from jax.experimental import pallas as pl
from jax.experimental.pallas import tpu as pltpu
from jax.sharding import PartitionSpec as P


CHUNK = 512
VMEM = pl.BlockSpec(memory_space=pltpu.VMEM)
SMEM = pl.BlockSpec(memory_space=pltpu.SMEM)
HBM = pl.BlockSpec(memory_space=pltpu.HBM)


def params(mib):
    return pltpu.CompilerParams(vmem_limit_bytes=int(mib * 1024 * 1024))


def shifted(values, steps):
    helpers = lax.axis_size("help")
    return lax.ppermute(values, "help", [(i, (i + steps) % helpers) for i in range(helpers)])


def pack_kernel(routing_ref, grad_ref, act_ref, send_ref, rows_ref, packed_ref, in_sems, out_sems):
    rows, (experts, slots, width) = grad_ref.shape[0], send_ref.shape
    loads, stores, base = [], [], 0
    for ref in (grad_ref, act_ref):
        for k in range(0, ref.shape[1], CHUNK):
            at = pl.ds(base + k, CHUNK)
            loads.append(pltpu.make_async_copy(ref.at[:, pl.ds(k, CHUNK)], rows_ref.at[:, at], in_sems.at[len(loads)]))
            stores.append(pltpu.make_async_copy(packed_ref.at[:, :, at], send_ref.at[:, :, at], out_sems.at[len(stores)]))
        base += ref.shape[1]
    for load in loads:
        load.start()
    across = jnp.broadcast_to(routing_ref[...], (rows, rows))
    first, second = (lax.broadcasted_iota(jnp.int32, (rows, rows), axis) for axis in (0, 1))
    earlier = jnp.where((across.T == across) & (first < second), 1.0, 0.0)
    target = routing_ref[...] * slots + jnp.sum(earlier, axis=0, keepdims=True).astype(jnp.int32)
    slot = lax.broadcasted_iota(jnp.int32, (experts * slots, rows), 0)
    pick = jnp.where(slot == target, 1.0, 0.0).astype(jnp.bfloat16)
    for i, k in enumerate(range(0, width, CHUNK)):
        loads[i].wait()
        taken = jnp.dot(pick, rows_ref[:, k : k + CHUNK], preferred_element_type=jnp.float32)
        packed_ref[:, :, k : k + CHUNK] = taken.astype(jnp.bfloat16).reshape(experts, slots, CHUNK)
        stores[i].start()
    for store in stores:
        store.wait()


def squares_of(arrived_ref, panel_ref, held_ref, sems, base):
    rows, depth = arrived_ref.shape[0] * arrived_ref.shape[1], panel_ref.shape[0]
    loads = [
        pltpu.make_async_copy(panel_ref.at[pl.ds(k, CHUNK), :], held_ref.at[pl.ds(k, CHUNK), :], sems.at[s])
        for s, k in enumerate(range(0, depth, CHUNK))
    ]
    for load in loads:
        load.start()
    total = None
    for load, k in zip(loads, range(0, depth, CHUNK)):
        values = arrived_ref[:, :, base + k : base + k + CHUNK].reshape(rows, CHUNK)
        load.wait()
        term = jnp.dot(values, held_ref[k : k + CHUNK, :], preferred_element_type=jnp.float32)
        total = term if total is None else total + term
    return jnp.square(total).astype(jnp.bfloat16)


def input_kernel(base, arrived_ref, panel_ref, squares_ref, held_ref, sems):
    squares_ref[...] = squares_of(arrived_ref, panel_ref, held_ref, sems, base)


def output_kernel(me_ref, arrived_ref, panel_ref, squares_ref, held_ref, sems):
    helpers, _, width = squares_ref.shape
    squares = squares_of(arrived_ref, panel_ref, held_ref, sems, 0)
    for k in range(helpers):
        squares_ref[lax.rem(me_ref[0] + helpers - k, helpers)] = squares[:, k * width : (k + 1) * width]


def tile_kernel(helpers, me_ref, *refs):
    in_refs, out_ref, tile_ref = refs[:helpers], refs[-2], refs[-1]
    width = tile_ref.shape[1] // helpers
    me = me_ref[0]
    for j in range(helpers):
        total = None
        for k in range(helpers):
            block = (j + k) % helpers
            term = lax.dot_general(
                in_refs[k][:, block * width : (block + 1) * width],
                out_ref[lax.rem(me + k, helpers)],
                (((0,), (0,)), ((), ())),
                preferred_element_type=jnp.float32,
            )
            total = term if total is None else total + term
        start = pl.multiple_of(lax.rem(me + helpers - j, helpers) * width, width)
        tile_ref[0, pl.ds(start, width), :] = total


def on_device(act_rows, grad_rows, routing, input_panel, output_panel):
    experts, helpers = lax.axis_size("expert"), lax.axis_size("help")
    (row_count, width_in), width_out = act_rows.shape, grad_rows.shape[1]
    part_in, part_out = input_panel.shape[2], output_panel.shape[2]
    panel_in = part_in * helpers
    chunks, slots = (width_in + width_out) // CHUNK, 2

    send = pl.pallas_call(
        pack_kernel,
        out_shape=jax.ShapeDtypeStruct((experts, slots, width_in + width_out), jnp.bfloat16),
        in_specs=[VMEM, HBM, HBM],
        out_specs=HBM,
        scratch_shapes=[
            pltpu.VMEM((row_count, width_in + width_out), jnp.bfloat16),
            pltpu.VMEM((experts, slots, width_in + width_out), jnp.bfloat16),
            pltpu.SemaphoreType.DMA((chunks,)),
            pltpu.SemaphoreType.DMA((chunks,)),
        ],
        compiler_params=params(62),
        name="pack",
    )(routing[None, :], grad_rows, act_rows)
    arrived = lax.all_to_all(send, "expert", split_axis=0, concat_axis=0, tiled=True)

    in_parts = [input_panel[0]] + [shifted(input_panel[0], k) for k in range(1, helpers)]
    out_parts = [output_panel[0]] + [shifted(output_panel[0], k) for k in range(1, helpers)]
    joined_in, joined_out = jnp.concatenate(in_parts, axis=1), jnp.concatenate(out_parts, axis=1)
    joined_in, joined_out, arrived = lax.optimization_barrier((joined_in, joined_out, arrived))

    own_in = pl.pallas_call(
        functools.partial(input_kernel, width_out),
        out_shape=jax.ShapeDtypeStruct((slots * experts, panel_in), jnp.bfloat16),
        in_specs=[VMEM, HBM],
        out_specs=VMEM,
        scratch_shapes=[
            pltpu.VMEM((width_in, panel_in), jnp.bfloat16),
            pltpu.SemaphoreType.DMA((width_in // CHUNK,)),
        ],
        compiler_params=params(12),
        name="input_squares",
    )(arrived, pltpu.with_memory_space_constraint(joined_in, pltpu.HBM))
    all_in = [own_in] + [shifted(own_in, helpers - k) for k in range(1, helpers)]

    me = lax.axis_index("help").astype(jnp.int32)[None]
    own_out = pl.pallas_call(
        output_kernel,
        out_shape=jax.ShapeDtypeStruct((helpers, slots * experts, part_out), jnp.bfloat16),
        in_specs=[SMEM, VMEM, HBM],
        out_specs=VMEM,
        scratch_shapes=[
            pltpu.VMEM((width_out, part_out * helpers), jnp.bfloat16),
            pltpu.SemaphoreType.DMA((width_out // CHUNK,)),
        ],
        compiler_params=params(16),
        cost_estimate=pl.CostEstimate(
            flops=2 * slots * experts * width_out * part_out * helpers,
            bytes_accessed=2 * width_out * part_out * helpers,
            transcendentals=0,
        ),
        name="output_squares",
    )(me, arrived, pltpu.with_memory_space_constraint(joined_out, pltpu.HBM))
    all_out = lax.all_to_all(own_out, "help", split_axis=0, concat_axis=0, tiled=True)

    return pl.pallas_call(
        functools.partial(tile_kernel, helpers),
        out_shape=jax.ShapeDtypeStruct((1, panel_in, part_out), jnp.float32),
        in_specs=[SMEM] + [VMEM] * (helpers + 1),
        out_specs=VMEM,
        compiler_params=params(12),
        name="tile",
    )(me, *all_in, all_out)


def solution(mesh):
    placed = (
        P(("expert", "help"), None),
        P(("expert", "help"), None),
        P(("expert", "help")),
        P("expert", None, "help"),
        P("expert", None, "help"),
    )
    return jax.shard_map(
        on_device, mesh=mesh, in_specs=placed, out_specs=P("expert", None, "help"), check_vma=False
    )
```

```python
import functools

import jax
import jax.numpy as jnp
from jax import lax
from jax.experimental import pallas as pl
from jax.experimental.pallas import tpu as pltpu
from jax.sharding import PartitionSpec as P


CHUNK = 512
VMEM = pl.BlockSpec(memory_space=pltpu.VMEM)
SMEM = pl.BlockSpec(memory_space=pltpu.SMEM)
HBM = pl.BlockSpec(memory_space=pltpu.HBM)


def params(mib):
    return pltpu.CompilerParams(vmem_limit_bytes=int(mib * 1024 * 1024))


def shifted(values, steps):
    helpers = lax.axis_size("help")
    return lax.ppermute(values, "help", [(i, (i + steps) % helpers) for i in range(helpers)])


def pack_kernel(routing_ref, grad_ref, act_ref, send_ref, rows_ref, packed_ref, in_sems, out_sems):
    rows, (experts, slots, _) = grad_ref.shape[0], send_ref.shape
    loads, stores, steps, base = [], [], [], 0
    for ref in (grad_ref, act_ref):
        for k in range(0, ref.shape[1], 2 * CHUNK):
            size = min(2 * CHUNK, ref.shape[1] - k)
            at = pl.ds(base + k, size)
            loads.append(pltpu.make_async_copy(ref.at[:, pl.ds(k, size)], rows_ref.at[:, at], in_sems.at[len(loads)]))
            stores.append(pltpu.make_async_copy(packed_ref.at[:, :, at], send_ref.at[:, :, at], out_sems.at[len(stores)]))
            steps.append((base + k, size))
        base += ref.shape[1]
    for load in loads:
        load.start()
    across = jnp.broadcast_to(routing_ref[...], (rows, rows))
    first, second = (lax.broadcasted_iota(jnp.int32, (rows, rows), axis) for axis in (0, 1))
    earlier = jnp.where((across.T == across) & (first < second), 1.0, 0.0)
    target = routing_ref[...] * slots + jnp.sum(earlier, axis=0, keepdims=True).astype(jnp.int32)
    slot = lax.broadcasted_iota(jnp.int32, (experts * slots, rows), 0)
    pick = jnp.where(slot == target, 1.0, 0.0).astype(jnp.bfloat16)
    for i, (k, size) in enumerate(steps):
        loads[i].wait()
        taken = jnp.dot(pick, rows_ref[:, k : k + size], preferred_element_type=jnp.float32)
        packed_ref[:, :, k : k + size] = taken.astype(jnp.bfloat16).reshape(experts, slots, size)
        stores[i].start()
    for store in stores:
        store.wait()


def squares_of(arrived_ref, panel_ref, held_ref, sems, base):
    rows, depth = arrived_ref.shape[0] * arrived_ref.shape[1], panel_ref.shape[0]
    loads = [
        pltpu.make_async_copy(panel_ref.at[pl.ds(k, CHUNK), :], held_ref.at[pl.ds(k, CHUNK), :], sems.at[s])
        for s, k in enumerate(range(0, depth, CHUNK))
    ]
    for load in loads:
        load.start()
    total = None
    for load, k in zip(loads, range(0, depth, CHUNK)):
        values = arrived_ref[:, :, base + k : base + k + CHUNK].reshape(rows, CHUNK)
        load.wait()
        term = jnp.dot(values, held_ref[k : k + CHUNK, :], preferred_element_type=jnp.float32)
        total = term if total is None else total + term
    return jnp.square(total).astype(jnp.bfloat16)


def input_kernel(base, arrived_ref, panel_ref, squares_ref, held_ref, own_ref, sems, out_sems):
    own_ref[...] = squares_of(arrived_ref, panel_ref, held_ref, sems, base)
    copies = [pltpu.make_async_copy(own_ref, squares_ref.at[k], out_sems.at[k]) for k in range(squares_ref.shape[0])]
    for copy in copies:
        copy.start()
    for copy in copies:
        copy.wait()


def output_kernel(arrived_ref, panel_ref, *refs):
    squares_refs, (held_ref, sems) = refs[:-2], refs[-2:]
    squares = squares_of(arrived_ref, panel_ref, held_ref, sems, 0)
    for k, ref in enumerate(squares_refs):
        ref[...] = squares[:, k * ref.shape[1] : (k + 1) * ref.shape[1]]


def tile_kernel(helpers, me_ref, in_ref, *refs):
    out_refs, tile_ref = refs[:-1], refs[-1]
    width = tile_ref.shape[1] // helpers
    me = me_ref[0]
    for j in range(helpers):
        total = None
        for k in range(helpers):
            block = (j + k) % helpers
            term = lax.dot_general(
                in_ref[lax.rem(me + k, helpers), :, block * width : (block + 1) * width],
                out_refs[k][...],
                (((0,), (0,)), ((), ())),
                preferred_element_type=jnp.float32,
            )
            total = term if total is None else total + term
        start = pl.multiple_of(lax.rem(me + helpers - j, helpers) * width, width)
        tile_ref[0, pl.ds(start, width), :] = total


def on_device(act_rows, grad_rows, routing, input_panel, output_panel):
    experts, helpers = lax.axis_size("expert"), lax.axis_size("help")
    (row_count, width_in), width_out = act_rows.shape, grad_rows.shape[1]
    part_in, part_out = input_panel.shape[2], output_panel.shape[2]
    panel_in = part_in * helpers
    chunks, slots = (width_in + width_out) // CHUNK, 2

    send = pl.pallas_call(
        pack_kernel,
        out_shape=jax.ShapeDtypeStruct((experts, slots, width_in + width_out), jnp.bfloat16),
        in_specs=[VMEM, HBM, HBM],
        out_specs=HBM,
        scratch_shapes=[
            pltpu.VMEM((row_count, width_in + width_out), jnp.bfloat16),
            pltpu.VMEM((experts, slots, width_in + width_out), jnp.bfloat16),
            pltpu.SemaphoreType.DMA((chunks,)),
            pltpu.SemaphoreType.DMA((chunks,)),
        ],
        compiler_params=params(62),
        name="pack",
    )(routing[None, :], grad_rows, act_rows)
    arrived = lax.all_to_all(send, "expert", split_axis=0, concat_axis=0, tiled=True)

    in_parts = [input_panel[0]] + [shifted(input_panel[0], k) for k in range(1, helpers)]
    out_parts = [output_panel[0]] + [shifted(output_panel[0], k) for k in range(1, helpers)]
    joined_in, joined_out = jnp.concatenate(in_parts, axis=1), jnp.concatenate(out_parts, axis=1)
    joined_in, joined_out, arrived = lax.optimization_barrier((joined_in, joined_out, arrived))

    own_in = pl.pallas_call(
        functools.partial(input_kernel, width_out),
        out_shape=pltpu.HBM((helpers, slots * experts, panel_in), jnp.bfloat16),
        in_specs=[VMEM, HBM],
        out_specs=HBM,
        scratch_shapes=[
            pltpu.VMEM((width_in, panel_in), jnp.bfloat16),
            pltpu.VMEM((slots * experts, panel_in), jnp.bfloat16),
            pltpu.SemaphoreType.DMA((width_in // CHUNK,)),
            pltpu.SemaphoreType.DMA((helpers,)),
        ],
        compiler_params=params(12),
        name="input_squares",
    )(arrived, pltpu.with_memory_space_constraint(joined_in, pltpu.HBM))
    all_in = lax.all_to_all(own_in, "help", split_axis=0, concat_axis=0, tiled=True)

    me = lax.axis_index("help").astype(jnp.int32)[None]
    own_out = pl.pallas_call(
        output_kernel,
        out_shape=[jax.ShapeDtypeStruct((slots * experts, part_out), jnp.bfloat16)] * helpers,
        in_specs=[VMEM, HBM],
        out_specs=[VMEM] * helpers,
        scratch_shapes=[
            pltpu.VMEM((width_out, part_out * helpers), jnp.bfloat16),
            pltpu.SemaphoreType.DMA((width_out // CHUNK,)),
        ],
        compiler_params=params(16),
        cost_estimate=pl.CostEstimate(
            flops=2 * slots * experts * width_out * part_out * helpers,
            bytes_accessed=2 * width_out * part_out * helpers,
            transcendentals=0,
        ),
        name="output_squares",
    )(arrived, pltpu.with_memory_space_constraint(joined_out, pltpu.HBM))
    all_out = [own_out[0]] + [shifted(own_out[k], helpers - k) for k in range(1, helpers)]

    return pl.pallas_call(
        functools.partial(tile_kernel, helpers),
        out_shape=jax.ShapeDtypeStruct((1, panel_in, part_out), jnp.float32),
        in_specs=[SMEM] + [VMEM] * (helpers + 1),
        out_specs=VMEM,
        compiler_params=params(12),
        name="tile",
    )(me, all_in, *all_out)


def solution(mesh):
    placed = (
        P(("expert", "help"), None),
        P(("expert", "help"), None),
        P(("expert", "help")),
        P("expert", None, "help"),
        P("expert", None, "help"),
    )
    return jax.shard_map(
        on_device, mesh=mesh, in_specs=placed, out_specs=P("expert", None, "help"), check_vma=False
    )
```

```python
import functools

import jax
import jax.numpy as jnp
from jax import lax
from jax.experimental import pallas as pl
from jax.experimental.pallas import tpu as pltpu
from jax.sharding import PartitionSpec as P


CHUNK = 512
VMEM = pl.BlockSpec(memory_space=pltpu.VMEM)
SMEM = pl.BlockSpec(memory_space=pltpu.SMEM)
HBM = pl.BlockSpec(memory_space=pltpu.HBM)


def params(mib):
    return pltpu.CompilerParams(vmem_limit_bytes=int(mib * 1024 * 1024))


def shifted(values, steps):
    helpers = lax.axis_size("help")
    return lax.ppermute(values, "help", [(i, (i + steps) % helpers) for i in range(helpers)])


def pack_kernel(routing_ref, grad_ref, act_ref, send_ref, rows_ref, packed_ref, in_sems, out_sems):
    rows, (experts, slots, _) = grad_ref.shape[0], send_ref.shape
    loads, stores, steps, base = [], [], [], 0
    for ref in (grad_ref, act_ref):
        for k in range(0, ref.shape[1], 2 * CHUNK):
            size = min(2 * CHUNK, ref.shape[1] - k)
            at = pl.ds(base + k, size)
            loads.append(pltpu.make_async_copy(ref.at[:, pl.ds(k, size)], rows_ref.at[:, at], in_sems.at[len(loads)]))
            stores.append(pltpu.make_async_copy(packed_ref.at[:, :, at], send_ref.at[:, :, at], out_sems.at[len(stores)]))
            steps.append((base + k, size))
        base += ref.shape[1]
    for load in loads:
        load.start()
    across = jnp.broadcast_to(routing_ref[...], (rows, rows))
    first, second = (lax.broadcasted_iota(jnp.int32, (rows, rows), axis) for axis in (0, 1))
    earlier = jnp.where((across.T == across) & (first < second), 1.0, 0.0)
    target = routing_ref[...] * slots + jnp.sum(earlier, axis=0, keepdims=True).astype(jnp.int32)
    slot = lax.broadcasted_iota(jnp.int32, (experts * slots, rows), 0)
    pick = jnp.where(slot == target, 1.0, 0.0).astype(jnp.bfloat16)
    for i, (k, size) in enumerate(steps):
        loads[i].wait()
        taken = jnp.dot(pick, rows_ref[:, k : k + size], preferred_element_type=jnp.float32)
        packed_ref[:, :, k : k + size] = taken.astype(jnp.bfloat16).reshape(experts, slots, size)
        stores[i].start()
    for store in stores:
        store.wait()


def squares_of(arrived_ref, panel_ref, held_ref, sems, base):
    rows, depth = arrived_ref.shape[0] * arrived_ref.shape[1], panel_ref.shape[0]
    loads = [
        pltpu.make_async_copy(panel_ref.at[pl.ds(k, CHUNK), :], held_ref.at[pl.ds(k, CHUNK), :], sems.at[s])
        for s, k in enumerate(range(0, depth, CHUNK))
    ]
    for load in loads:
        load.start()
    total = None
    for load, k in zip(loads, range(0, depth, CHUNK)):
        values = arrived_ref[:, :, base + k : base + k + CHUNK].reshape(rows, CHUNK)
        load.wait()
        term = jnp.dot(values, held_ref[k : k + CHUNK, :], preferred_element_type=jnp.float32)
        total = term if total is None else total + term
    return jnp.square(total).astype(jnp.bfloat16)


def input_kernel(base, arrived_ref, panel_ref, squares_ref, held_ref, own_ref, sems, out_sems):
    own_ref[...] = squares_of(arrived_ref, panel_ref, held_ref, sems, base)
    copies = [pltpu.make_async_copy(own_ref, squares_ref.at[k], out_sems.at[k]) for k in range(squares_ref.shape[0])]
    for copy in copies:
        copy.start()
    for copy in copies:
        copy.wait()


def output_kernel(arrived_ref, panel_ref, *refs):
    squares_refs, (held_ref, sems) = refs[:-2], refs[-2:]
    squares = squares_of(arrived_ref, panel_ref, held_ref, sems, 0)
    for k, ref in enumerate(squares_refs):
        ref[...] = squares[:, k * ref.shape[1] : (k + 1) * ref.shape[1]]


def tile_kernel(helpers, me_ref, in_ref, *refs):
    out_refs, (tile_ref, held_ref, sems) = refs[:helpers], refs[helpers:]
    width = tile_ref.shape[1] // helpers
    me = me_ref[0]
    loads = [
        pltpu.make_async_copy(in_ref.at[lax.rem(me + k, helpers)], held_ref.at[k], sems.at[k]) for k in range(helpers)
    ]
    for load in loads:
        load.start()
    totals = [None] * helpers
    for k in range(helpers):
        loads[k].wait()
        for j in range(helpers):
            block = (j + k) % helpers
            term = lax.dot_general(
                held_ref[k, :, block * width : (block + 1) * width],
                out_refs[k][...],
                (((0,), (0,)), ((), ())),
                preferred_element_type=jnp.float32,
            )
            totals[j] = term if totals[j] is None else totals[j] + term
    for j in range(helpers):
        start = pl.multiple_of(lax.rem(me + helpers - j, helpers) * width, width)
        tile_ref[0, pl.ds(start, width), :] = totals[j]


def on_device(act_rows, grad_rows, routing, input_panel, output_panel):
    experts, helpers = lax.axis_size("expert"), lax.axis_size("help")
    (row_count, width_in), width_out = act_rows.shape, grad_rows.shape[1]
    part_in, part_out = input_panel.shape[2], output_panel.shape[2]
    panel_in = part_in * helpers
    chunks, slots = (width_in + width_out) // CHUNK, 2

    send = pl.pallas_call(
        pack_kernel,
        out_shape=jax.ShapeDtypeStruct((experts, slots, width_in + width_out), jnp.bfloat16),
        in_specs=[VMEM, HBM, HBM],
        out_specs=HBM,
        scratch_shapes=[
            pltpu.VMEM((row_count, width_in + width_out), jnp.bfloat16),
            pltpu.VMEM((experts, slots, width_in + width_out), jnp.bfloat16),
            pltpu.SemaphoreType.DMA((chunks,)),
            pltpu.SemaphoreType.DMA((chunks,)),
        ],
        compiler_params=params(62),
        name="pack",
    )(routing[None, :], grad_rows, act_rows)
    arrived = lax.all_to_all(send, "expert", split_axis=0, concat_axis=0, tiled=True)

    in_parts = [input_panel[0]] + [shifted(input_panel[0], k) for k in range(1, helpers)]
    out_parts = [output_panel[0]] + [shifted(output_panel[0], k) for k in range(1, helpers)]
    joined_in, joined_out = jnp.concatenate(in_parts, axis=1), jnp.concatenate(out_parts, axis=1)
    joined_in, joined_out, arrived = lax.optimization_barrier((joined_in, joined_out, arrived))

    own_in = pl.pallas_call(
        functools.partial(input_kernel, width_out),
        out_shape=pltpu.HBM((helpers, slots * experts, panel_in), jnp.bfloat16),
        in_specs=[VMEM, HBM],
        out_specs=HBM,
        scratch_shapes=[
            pltpu.VMEM((width_in, panel_in), jnp.bfloat16),
            pltpu.VMEM((slots * experts, panel_in), jnp.bfloat16),
            pltpu.SemaphoreType.DMA((width_in // CHUNK,)),
            pltpu.SemaphoreType.DMA((helpers,)),
        ],
        compiler_params=params(12),
        name="input_squares",
    )(arrived, pltpu.with_memory_space_constraint(joined_in, pltpu.HBM))
    all_in = lax.all_to_all(own_in, "help", split_axis=0, concat_axis=0, tiled=True)

    me = lax.axis_index("help").astype(jnp.int32)[None]
    own_out = pl.pallas_call(
        output_kernel,
        out_shape=[jax.ShapeDtypeStruct((slots * experts, part_out), jnp.bfloat16)] * helpers,
        in_specs=[VMEM, HBM],
        out_specs=[VMEM] * helpers,
        scratch_shapes=[
            pltpu.VMEM((width_out, part_out * helpers), jnp.bfloat16),
            pltpu.SemaphoreType.DMA((width_out // CHUNK,)),
        ],
        compiler_params=params(16),
        cost_estimate=pl.CostEstimate(
            flops=2 * slots * experts * width_out * part_out * helpers,
            bytes_accessed=2 * width_out * part_out * helpers,
            transcendentals=0,
        ),
        name="output_squares",
    )(arrived, pltpu.with_memory_space_constraint(joined_out, pltpu.HBM))
    all_out = [own_out[0]]
    for k in range(1, helpers):
        all_out.append(shifted(own_out[k], helpers - k))

    return pl.pallas_call(
        functools.partial(tile_kernel, helpers),
        out_shape=jax.ShapeDtypeStruct((1, panel_in, part_out), jnp.float32),
        in_specs=[SMEM, HBM] + [VMEM] * helpers,
        out_specs=VMEM,
        scratch_shapes=[
            pltpu.VMEM((helpers, slots * experts, panel_in), jnp.bfloat16),
            pltpu.SemaphoreType.DMA((helpers,)),
        ],
        compiler_params=params(12),
        name="tile",
    )(me, pltpu.with_memory_space_constraint(all_in, pltpu.HBM), *all_out)


def solution(mesh):
    placed = (
        P(("expert", "help"), None),
        P(("expert", "help"), None),
        P(("expert", "help")),
        P("expert", None, "help"),
        P("expert", None, "help"),
    )
    return jax.shard_map(
        on_device, mesh=mesh, in_specs=placed, out_specs=P("expert", None, "help"), check_vma=False
    )
```

```python
import functools

import jax
import jax.numpy as jnp
from jax import lax
from jax.experimental import pallas as pl
from jax.experimental.pallas import tpu as pltpu
from jax.sharding import PartitionSpec as P


CHUNK = 512
VMEM = pl.BlockSpec(memory_space=pltpu.VMEM)
HBM = pl.BlockSpec(memory_space=pltpu.HBM)


def params(mib):
    return pltpu.CompilerParams(vmem_limit_bytes=int(mib * 1024 * 1024))


def shifted(values, steps):
    helpers = lax.axis_size("help")
    return lax.ppermute(values, "help", [(i, (i + steps) % helpers) for i in range(helpers)])


def pack_kernel(routing_hbm_ref, grad_ref, act_ref, send_ref, routing_ref, rows_ref, packed_ref, sem, in_sems, out_sems):
    rows, (experts, slots, _) = grad_ref.shape[0], send_ref.shape
    loads, stores, steps, base = [], [], [], 0
    for ref in (grad_ref, act_ref):
        for k in range(0, ref.shape[1], 2 * CHUNK):
            size = min(2 * CHUNK, ref.shape[1] - k)
            at = pl.ds(base + k, size)
            loads.append(pltpu.make_async_copy(ref.at[:, pl.ds(k, size)], rows_ref.at[:, at], in_sems.at[len(loads)]))
            stores.append(pltpu.make_async_copy(packed_ref.at[:, :, at], send_ref.at[:, :, at], out_sems.at[len(stores)]))
            steps.append((base + k, size))
        base += ref.shape[1]
    named = pltpu.make_async_copy(routing_hbm_ref, routing_ref, sem)
    named.start()
    for load in loads:
        load.start()
    named.wait()
    across = jnp.broadcast_to(routing_ref[...], (rows, rows))
    first, second = (lax.broadcasted_iota(jnp.int32, (rows, rows), axis) for axis in (0, 1))
    earlier = jnp.where((across.T == across) & (first < second), 1.0, 0.0)
    target = routing_ref[...] * slots + jnp.sum(earlier, axis=0, keepdims=True).astype(jnp.int32)
    slot = lax.broadcasted_iota(jnp.int32, (experts * slots, rows), 0)
    pick = jnp.where(slot == target, 1.0, 0.0).astype(jnp.bfloat16)
    for i, (k, size) in enumerate(steps):
        loads[i].wait()
        taken = jnp.dot(pick, rows_ref[:, k : k + size], preferred_element_type=jnp.float32)
        packed_ref[:, :, k : k + size] = taken.astype(jnp.bfloat16).reshape(experts, slots, size)
        stores[i].start()
    for store in stores:
        store.wait()


def squares_of(arrived_ref, panel_ref, held_ref, sems, base):
    rows, depth = arrived_ref.shape[0] * arrived_ref.shape[1], panel_ref.shape[0]
    loads = [
        pltpu.make_async_copy(panel_ref.at[pl.ds(k, CHUNK), :], held_ref.at[pl.ds(k, CHUNK), :], sems.at[s])
        for s, k in enumerate(range(0, depth, CHUNK))
    ]
    for load in loads:
        load.start()
    total = None
    for load, k in zip(loads, range(0, depth, CHUNK)):
        values = arrived_ref[:, :, base + k : base + k + CHUNK].reshape(rows, CHUNK)
        load.wait()
        term = jnp.dot(values, held_ref[k : k + CHUNK, :], preferred_element_type=jnp.float32)
        total = term if total is None else total + term
    return jnp.square(total).astype(jnp.bfloat16)


def input_kernel(base, arrived_ref, panel_ref, squares_ref, held_ref, own_ref, sems, out_sems):
    own_ref[...] = squares_of(arrived_ref, panel_ref, held_ref, sems, base)
    copies = [pltpu.make_async_copy(own_ref, squares_ref.at[k], out_sems.at[k]) for k in range(squares_ref.shape[0])]
    for copy in copies:
        copy.start()
    for copy in copies:
        copy.wait()


def output_kernel(arrived_ref, panel_ref, *refs):
    squares_refs, (held_ref, sems) = refs[:-2], refs[-2:]
    squares = squares_of(arrived_ref, panel_ref, held_ref, sems, 0)
    for k, ref in enumerate(squares_refs):
        ref[...] = squares[:, k * ref.shape[1] : (k + 1) * ref.shape[1]]


def tile_kernel(helpers, in_ref, *refs):
    out_refs, (tile_ref, held_ref, sems) = refs[:helpers], refs[helpers:]
    width = tile_ref.shape[1] // helpers
    me = lax.axis_index("help")
    loads = [
        pltpu.make_async_copy(in_ref.at[lax.rem(me + k, helpers)], held_ref.at[k], sems.at[k]) for k in range(helpers)
    ]
    for load in loads:
        load.start()
    totals = [None] * helpers
    for k in range(helpers):
        loads[k].wait()
        for j in range(helpers):
            block = (j + k) % helpers
            term = lax.dot_general(
                held_ref[k, :, block * width : (block + 1) * width],
                out_refs[k][...],
                (((0,), (0,)), ((), ())),
                preferred_element_type=jnp.float32,
            )
            totals[j] = term if totals[j] is None else totals[j] + term
    for j in range(helpers):
        start = pl.multiple_of(lax.rem(me + helpers - j, helpers) * width, width)
        tile_ref[0, pl.ds(start, width), :] = totals[j]


def on_device(act_rows, grad_rows, routing, input_panel, output_panel):
    experts, helpers = lax.axis_size("expert"), lax.axis_size("help")
    (row_count, width_in), width_out = act_rows.shape, grad_rows.shape[1]
    part_in, part_out = input_panel.shape[2], output_panel.shape[2]
    panel_in = part_in * helpers
    chunks, slots = (width_in + width_out) // CHUNK, 2

    send = pl.pallas_call(
        pack_kernel,
        out_shape=jax.ShapeDtypeStruct((experts, slots, width_in + width_out), jnp.bfloat16),
        in_specs=[HBM] * 3,
        out_specs=HBM,
        scratch_shapes=[
            pltpu.VMEM((1, row_count), jnp.int32),
            pltpu.VMEM((row_count, width_in + width_out), jnp.bfloat16),
            pltpu.VMEM((experts, slots, width_in + width_out), jnp.bfloat16),
            pltpu.SemaphoreType.DMA,
            pltpu.SemaphoreType.DMA((chunks,)),
            pltpu.SemaphoreType.DMA((chunks,)),
        ],
        compiler_params=params(62),
        name="pack",
    )(routing[None, :], grad_rows, act_rows)
    arrived = lax.all_to_all(send, "expert", split_axis=0, concat_axis=0, tiled=True)

    in_parts = [input_panel[0]] + [shifted(input_panel[0], k) for k in range(1, helpers)]
    out_parts = [output_panel[0]] + [shifted(output_panel[0], k) for k in range(1, helpers)]
    joined_in, joined_out = jnp.concatenate(in_parts, axis=1), jnp.concatenate(out_parts, axis=1)
    joined_in, joined_out, arrived = lax.optimization_barrier((joined_in, joined_out, arrived))

    own_in = pl.pallas_call(
        functools.partial(input_kernel, width_out),
        out_shape=pltpu.HBM((helpers, slots * experts, panel_in), jnp.bfloat16),
        in_specs=[VMEM, HBM],
        out_specs=HBM,
        scratch_shapes=[
            pltpu.VMEM((width_in, panel_in), jnp.bfloat16),
            pltpu.VMEM((slots * experts, panel_in), jnp.bfloat16),
            pltpu.SemaphoreType.DMA((width_in // CHUNK,)),
            pltpu.SemaphoreType.DMA((helpers,)),
        ],
        compiler_params=params(12),
        name="input_squares",
    )(arrived, pltpu.with_memory_space_constraint(joined_in, pltpu.HBM))
    all_in = lax.all_to_all(own_in, "help", split_axis=0, concat_axis=0, tiled=True)

    own_out = pl.pallas_call(
        output_kernel,
        out_shape=[jax.ShapeDtypeStruct((slots * experts, part_out), jnp.bfloat16)] * helpers,
        in_specs=[VMEM, HBM],
        out_specs=[VMEM] * helpers,
        scratch_shapes=[
            pltpu.VMEM((width_out, part_out * helpers), jnp.bfloat16),
            pltpu.SemaphoreType.DMA((width_out // CHUNK,)),
        ],
        compiler_params=params(16),
        cost_estimate=pl.CostEstimate(
            flops=2 * slots * experts * width_out * part_out * helpers,
            bytes_accessed=2 * width_out * part_out * helpers,
            transcendentals=0,
        ),
        name="output_squares",
    )(arrived, pltpu.with_memory_space_constraint(joined_out, pltpu.HBM))
    all_out = [own_out[0]]
    for k in range(1, helpers):
        all_out.append(shifted(own_out[k], helpers - k))

    return pl.pallas_call(
        functools.partial(tile_kernel, helpers),
        out_shape=jax.ShapeDtypeStruct((1, panel_in, part_out), jnp.float32),
        in_specs=[HBM] + [VMEM] * helpers,
        out_specs=VMEM,
        scratch_shapes=[
            pltpu.VMEM((helpers, slots * experts, panel_in), jnp.bfloat16),
            pltpu.SemaphoreType.DMA((helpers,)),
        ],
        compiler_params=params(12),
        name="tile",
    )(pltpu.with_memory_space_constraint(all_in, pltpu.HBM), *all_out)


def solution(mesh):
    placed = (
        P(("expert", "help"), None),
        P(("expert", "help"), None),
        P(("expert", "help")),
        P("expert", None, "help"),
        P("expert", None, "help"),
    )
    return jax.shard_map(
        on_device, mesh=mesh, in_specs=placed, out_specs=P("expert", None, "help"), check_vma=False
    )
```

```python
import functools

import jax
import jax.numpy as jnp
from jax import lax
from jax.experimental import pallas as pl
from jax.experimental.pallas import tpu as pltpu
from jax.sharding import PartitionSpec as P


CHUNK = 512
VMEM = pl.BlockSpec(memory_space=pltpu.VMEM)
HBM = pl.BlockSpec(memory_space=pltpu.HBM)


def params(mib):
    return pltpu.CompilerParams(vmem_limit_bytes=int(mib * 1024 * 1024))


def shifted(values, steps):
    helpers = lax.axis_size("help")
    return lax.ppermute(values, "help", [(i, (i + steps) % helpers) for i in range(helpers)])


def pack_kernel(routing_hbm_ref, grad_ref, act_ref, send_ref, routing_ref, rows_ref, packed_ref, sem, in_sems, out_sems):
    rows, (experts, slots, _) = grad_ref.shape[0], send_ref.shape
    loads, stores, steps, base = [], [], [], 0
    for ref in (grad_ref, act_ref):
        for k in range(0, ref.shape[1], 2 * CHUNK):
            size = min(2 * CHUNK, ref.shape[1] - k)
            at = pl.ds(base + k, size)
            loads.append(pltpu.make_async_copy(ref.at[:, pl.ds(k, size)], rows_ref.at[:, at], in_sems.at[len(loads)]))
            stores.append(pltpu.make_async_copy(packed_ref.at[:, :, at], send_ref.at[:, :, at], out_sems.at[len(stores)]))
            steps.append((base + k, size))
        base += ref.shape[1]
    named = pltpu.make_async_copy(routing_hbm_ref, routing_ref, sem)
    named.start()
    for load in loads:
        load.start()
    named.wait()
    across = jnp.broadcast_to(routing_ref[...], (rows, rows))
    first, second = (lax.broadcasted_iota(jnp.int32, (rows, rows), axis) for axis in (0, 1))
    earlier = jnp.where((across.T == across) & (first < second), 1.0, 0.0)
    target = routing_ref[...] * slots + jnp.sum(earlier, axis=0, keepdims=True).astype(jnp.int32)
    slot = lax.broadcasted_iota(jnp.int32, (experts * slots, rows), 0)
    pick = jnp.where(slot == target, 1.0, 0.0).astype(jnp.bfloat16)
    for i, (k, size) in enumerate(steps):
        loads[i].wait()
        taken = jnp.dot(pick, rows_ref[:, k : k + size], preferred_element_type=jnp.float32)
        packed_ref[:, :, k : k + size] = taken.astype(jnp.bfloat16).reshape(experts, slots, size)
        stores[i].start()
    for store in stores:
        store.wait()


def squares_of(arrived_ref, panel_ref, held_ref, sems, base):
    rows, depth = arrived_ref.shape[0] * arrived_ref.shape[1], panel_ref.shape[0]
    loads = [
        pltpu.make_async_copy(panel_ref.at[pl.ds(k, CHUNK), :], held_ref.at[pl.ds(k, CHUNK), :], sems.at[s])
        for s, k in enumerate(range(0, depth, CHUNK))
    ]
    for load in loads:
        load.start()
    total = None
    for load, k in zip(loads, range(0, depth, CHUNK)):
        values = arrived_ref[:, :, base + k : base + k + CHUNK].reshape(rows, CHUNK)
        load.wait()
        term = jnp.dot(values, held_ref[k : k + CHUNK, :], preferred_element_type=jnp.float32)
        total = term if total is None else total + term
    return jnp.square(total).astype(jnp.bfloat16)


def input_kernel(base, arrived_ref, panel_ref, squares_ref, held_ref, own_ref, sems, out_sems):
    own_ref[...] = squares_of(arrived_ref, panel_ref, held_ref, sems, base)
    copies = [pltpu.make_async_copy(own_ref, squares_ref.at[k], out_sems.at[k]) for k in range(squares_ref.shape[0])]
    for copy in copies:
        copy.start()
    for copy in copies:
        copy.wait()


def output_kernel(arrived_ref, panel_ref, *refs):
    squares_refs, (held_ref, sems) = refs[:-2], refs[-2:]
    squares = squares_of(arrived_ref, panel_ref, held_ref, sems, 0)
    for k, ref in enumerate(squares_refs):
        ref[...] = squares[:, k * ref.shape[1] : (k + 1) * ref.shape[1]]


def early_kernel(in_ref, held_ref, sems):
    copies = [pltpu.make_async_copy(in_ref.at[k], held_ref.at[k], sems.at[k]) for k in range(in_ref.shape[0])]
    for copy in copies:
        copy.start()
    for copy in copies:
        copy.wait()


def tile_kernel(helpers, in_ref, *refs):
    out_refs, tile_ref = refs[:-1], refs[-1]
    width = tile_ref.shape[1] // helpers
    me = lax.axis_index("help")
    for j in range(helpers):
        total = None
        for k in range(helpers):
            block = (j + k) % helpers
            term = lax.dot_general(
                in_ref[lax.rem(me + k, helpers), :, block * width : (block + 1) * width],
                out_refs[k][...],
                (((0,), (0,)), ((), ())),
                preferred_element_type=jnp.float32,
            )
            total = term if total is None else total + term
        start = pl.multiple_of(lax.rem(me + helpers - j, helpers) * width, width)
        tile_ref[0, pl.ds(start, width), :] = total


def on_device(act_rows, grad_rows, routing, input_panel, output_panel):
    experts, helpers = lax.axis_size("expert"), lax.axis_size("help")
    (row_count, width_in), width_out = act_rows.shape, grad_rows.shape[1]
    part_in, part_out = input_panel.shape[2], output_panel.shape[2]
    panel_in = part_in * helpers
    chunks, slots = (width_in + width_out) // CHUNK, 2

    send = pl.pallas_call(
        pack_kernel,
        out_shape=jax.ShapeDtypeStruct((experts, slots, width_in + width_out), jnp.bfloat16),
        in_specs=[HBM] * 3,
        out_specs=HBM,
        scratch_shapes=[
            pltpu.VMEM((1, row_count), jnp.int32),
            pltpu.VMEM((row_count, width_in + width_out), jnp.bfloat16),
            pltpu.VMEM((experts, slots, width_in + width_out), jnp.bfloat16),
            pltpu.SemaphoreType.DMA,
            pltpu.SemaphoreType.DMA((chunks,)),
            pltpu.SemaphoreType.DMA((chunks,)),
        ],
        compiler_params=params(62),
        name="pack",
    )(routing[None, :], grad_rows, act_rows)
    arrived = lax.all_to_all(send, "expert", split_axis=0, concat_axis=0, tiled=True)

    in_parts = [input_panel[0]] + [shifted(input_panel[0], k) for k in range(1, helpers)]
    out_parts = [output_panel[0]] + [shifted(output_panel[0], k) for k in range(1, helpers)]
    joined_in, joined_out = jnp.concatenate(in_parts, axis=1), jnp.concatenate(out_parts, axis=1)
    joined_in, joined_out, arrived = lax.optimization_barrier((joined_in, joined_out, arrived))

    own_in = pl.pallas_call(
        functools.partial(input_kernel, width_out),
        out_shape=pltpu.HBM((helpers, slots * experts, panel_in), jnp.bfloat16),
        in_specs=[VMEM, HBM],
        out_specs=HBM,
        scratch_shapes=[
            pltpu.VMEM((width_in, panel_in), jnp.bfloat16),
            pltpu.VMEM((slots * experts, panel_in), jnp.bfloat16),
            pltpu.SemaphoreType.DMA((width_in // CHUNK,)),
            pltpu.SemaphoreType.DMA((helpers,)),
        ],
        compiler_params=params(12),
        name="input_squares",
    )(arrived, pltpu.with_memory_space_constraint(joined_in, pltpu.HBM))
    all_in = lax.all_to_all(own_in, "help", split_axis=0, concat_axis=0, tiled=True)

    own_out = pl.pallas_call(
        output_kernel,
        out_shape=[jax.ShapeDtypeStruct((slots * experts, part_out), jnp.bfloat16)] * helpers,
        in_specs=[VMEM, HBM],
        out_specs=[VMEM] * helpers,
        scratch_shapes=[
            pltpu.VMEM((width_out, part_out * helpers), jnp.bfloat16),
            pltpu.SemaphoreType.DMA((width_out // CHUNK,)),
        ],
        compiler_params=params(16),
        cost_estimate=pl.CostEstimate(
            flops=2 * slots * experts * width_out * part_out * helpers,
            bytes_accessed=2 * width_out * part_out * helpers,
            transcendentals=0,
        ),
        name="output_squares",
    )(arrived, pltpu.with_memory_space_constraint(joined_out, pltpu.HBM))
    all_out = [own_out[0]]
    for k in range(1, helpers):
        all_out.append(shifted(own_out[k], helpers - k))

    all_in = pl.pallas_call(
        early_kernel,
        out_shape=jax.ShapeDtypeStruct(all_in.shape, all_in.dtype),
        in_specs=[HBM],
        out_specs=VMEM,
        scratch_shapes=[pltpu.SemaphoreType.DMA((helpers,))],
        compiler_params=params(8),
        name="early",
    )(pltpu.with_memory_space_constraint(all_in, pltpu.HBM))
    return pl.pallas_call(
        functools.partial(tile_kernel, helpers),
        out_shape=jax.ShapeDtypeStruct((1, panel_in, part_out), jnp.float32),
        in_specs=[VMEM] * (helpers + 1),
        out_specs=VMEM,
        compiler_params=params(12),
        name="tile",
    )(all_in, *all_out)


def solution(mesh):
    placed = (
        P(("expert", "help"), None),
        P(("expert", "help"), None),
        P(("expert", "help")),
        P("expert", None, "help"),
        P("expert", None, "help"),
    )
    return jax.shard_map(
        on_device, mesh=mesh, in_specs=placed, out_specs=P("expert", None, "help"), check_vma=False
    )
```
